32 devices in a mesh: seq: 8 (over z, core), mp: 2 (over x), dp: 2 (over y).
Axes of the slice: x: 2, y: 2, z: 4, core: 2. Of those that a mesh axis runs over, the one named last changes fastest.
Arguments:
- x_enc: bfloat16 [8192, 3072], P(('dp', 'seq')), parts along dimension 0, may hold values from -6 to 6
- clip_blocks: int32 [16], P('dp'), parts along dimension 0, may hold values from 1 to 40, 64 in all
- timesteps: int32 [16], P('dp'), parts along dimension 0, may hold values from 0 to 999
- plan_block: int32 [16, 8], P(('dp', 'seq')), parts along dimension 0, may hold values from 0 to 7, each once within a row
- plan_slot: int32 [16, 8], P(('dp', 'seq')), parts along dimension 0, may hold values from 0 to 7, each once within a row
- t_weight: bfloat16 [256, 3072], replicated, may hold values from -0.375 to 0.375
- ada_weight: bfloat16 [3072, 9216], P(('seq', 'mp')), may hold values from -0.4375 to 0.4375
- w_qkv: bfloat16 [3072, 3, 3072], P(None, None, 'mp'), may hold values from -0.109375 to 0.109375
- w_out: bfloat16 [3072, 3072], P('mp'), may hold values from -0.109375 to 0.109375
Outputs:
- update: bfloat16 [8192, 3072], P(('dp', 'seq', 'mp')), parts along dimension 0
- mixed: bfloat16 [8192, 3072], P(('dp', 'seq', 'mp')), parts along dimension 0
The draws below stay inside these ranges and needn't reach their ends.
There are 2 independent parts, one for each index of `dp`. The reference program is written for one: setup_inputs(seed, part) draws one part's arguments, and reference() takes and returns one part's arrays. A program takes and returns all parts, laid end to end along the dimension named above; an argument that names none is the same for every part. Nothing has to cross between parts.
Inputs may be any that keep to these rules, and one draw needn't show every extreme that they name: Each row of plan_block is a permutation of 0 to 7. Each row of plan_slot is a permutation of 0 to 7. `clip_blocks`: the entries sum to 64; the longest clip has exactly 40 blocks.
All inputs are finite; a program needn't handle non-finite values.
Results may differ from the reference program's by a relative error of at most 0.02.
Values may be sent and summed in bfloat16 or wider, within the bound.
No kernel may reach another device: no remote copies, remote signals or barrier semaphores. Data moves between devices by JAX's collectives and lax.ppermute only.
A program may use at most 192 MiB of HBM per device.

```python
import math
import jax
import jax.numpy as jnp
import numpy as np
from jax import lax

D = 3072
HEADS = 24
HEAD = 128
TFREQ = 256
CLIPS = 8
S_DEV = 512
BLK = 64
NBLK = 64
MOST = 40
TOKENS = 4096
N_SEQ = 8


def touch_ends(entries, own_key, low, high):
    place = [jax.random.randint(jax.random.fold_in(own_key, axis), (), 0, length) for axis, length in enumerate(entries.shape)]
    widest = entries.shape.index(max(entries.shape))
    beside = place[:widest] + [(place[widest] + 1) % entries.shape[widest]] + place[widest + 1:]
    return entries.at[tuple(place)].set(low).at[tuple(beside)].set(high)


def shard_levels(rng, extent, cuts, least, high):
    gain = 1.0
    for axis_at, shards_of in cuts:
        steps = jax.random.uniform(jax.random.fold_in(jax.random.fold_in(rng, 6), axis_at), (shards_of,), jnp.float32, least / len(cuts), high / len(cuts))
        gain = gain * jnp.repeat(jnp.exp(steps), extent[axis_at] // shards_of).reshape((-1,) + (1,) * (len(extent) - 1 - axis_at))
    return gain


def profile(count, total, reach, skew):
    weights = [(1 << 20) // math.isqrt(standing ** skew) + 1 for standing in range(2, count + 1)]
    rest, holding = total - reach - (count - 1), [1] * (count - 1)
    while rest > 0:
        movable = [i for i in range(count - 1) if holding[i] < reach]
        whole, remaining = sum([weights[i] for i in movable]), rest
        for i in movable:
            addition = min(reach - holding[i], max(1, remaining * weights[i] // whole), rest)
            holding[i] = holding[i] + addition
            rest = rest - addition
    return np.array([reach] + holding)


def uneven(stream_key, number_of, total, limit, lean):
    if number_of == 2:
        one = jax.random.randint(stream_key, (), max(1, total - limit), min(limit, total - 1) + 1)
        return jnp.stack([one, total - one])
    sizes = jnp.asarray(profile(number_of, total, limit, lean), jnp.int32)
    twos = (number_of - 1) // 2
    source_of, receiver = sizes[1:1 + 2 * twos:2], sizes[2:2 + 2 * twos:2]
    slack = jnp.minimum(source_of - 1, limit - receiver)
    moved = jax.random.randint(jax.random.fold_in(stream_key, 1), (twos,), 0, 1 << 20) % (slack + 1)
    sizes = sizes.at[1:1 + 2 * twos:2].set(source_of - moved).at[2:2 + 2 * twos:2].set(receiver + moved)
    return sizes[jax.random.permutation(jax.random.fold_in(stream_key, 2), number_of)]


def centred(rng, shape, scale, reach, split=(), kind=jnp.bfloat16):
    gain = shard_levels(rng, shape, split, -0.22, 0.18) if split else 1.0
    values = jax.random.normal(rng, shape, jnp.float32) * scale * gain
    return jnp.minimum(jnp.maximum(values, -reach), reach).astype(kind)


def setup_inputs(seed: int = 0, part: int = 0) -> dict:
    seeds = jax.random.split(jax.random.key(seed), 10)
    part_keys = jax.random.split(jax.random.fold_in(seeds[9], part), 10)
    x_enc = centred(part_keys[0], (TOKENS, D), 1.0, 6.0, ((0, 8),))
    clip_blocks = uneven(part_keys[1], CLIPS, NBLK, MOST, 2).astype(jnp.int32)
    timesteps = touch_ends(jax.random.randint(part_keys[2], (CLIPS,), 0, 1000), jax.random.fold_in(part_keys[2], 1), 0, 999).astype(jnp.int32)
    plan_block = jax.vmap(lambda own: jax.random.permutation(own, N_SEQ))(jax.random.split(part_keys[3], N_SEQ)).reshape((N_SEQ, N_SEQ)).astype(jnp.int32)
    plan_slot = jax.vmap(lambda own: jax.random.permutation(own, N_SEQ))(jax.random.split(part_keys[4], N_SEQ)).reshape((N_SEQ, N_SEQ)).astype(jnp.int32)
    t_weight = centred(seeds[5], (TFREQ, D), TFREQ ** -0.5, 0.375)
    ada_weight = centred(seeds[6], (D, 3 * D), (D // 16) ** -0.5, 0.4375, ((0, 16),))
    w_qkv = centred(seeds[7], (D, 3, D), D ** -0.5, 0.109375, ((2, 2),))
    w_out = centred(seeds[8], (D, D), D ** -0.5, 0.109375, ((0, 2),))
    return dict(x_enc=x_enc, clip_blocks=clip_blocks, timesteps=timesteps, plan_block=plan_block, plan_slot=plan_slot, t_weight=t_weight, ada_weight=ada_weight, w_qkv=w_qkv, w_out=w_out)


def clip_ids(clip_blocks, count):
    ends = jnp.cumsum(clip_blocks).astype(jnp.int32)
    block = (jnp.arange(count, dtype=jnp.int32) // BLK).astype(jnp.int32)
    return lax.optimization_barrier(jnp.sum((block[:, None] >= ends[None, :]).astype(jnp.int32), axis=1)).astype(jnp.int32)

def reference(x_enc, clip_blocks, timesteps, plan_block, plan_slot, t_weight, ada_weight, w_qkv, w_out):
    grid_d, grid_s = jnp.meshgrid(jnp.arange(N_SEQ, dtype=jnp.int32), jnp.arange(N_SEQ, dtype=jnp.int32), indexing='ij')
    slot = plan_slot[grid_d, grid_s]
    block = plan_block[grid_s, grid_d]
    src_s = jnp.zeros((N_SEQ, N_SEQ), jnp.int32).at[grid_d, slot].set(grid_s)
    src_b = jnp.zeros((N_SEQ, N_SEQ), jnp.int32).at[grid_d, slot].set(block)
    blocks = x_enc.reshape(N_SEQ, N_SEQ, BLK, D)
    packed = blocks[src_s, src_b].reshape(TOKENS, D)
    clip_tok = clip_ids(clip_blocks, TOKENS)
    half = TFREQ // 2
    freqs = jnp.exp(-math.log(10000.0) * jnp.arange(half, dtype=jnp.float32) / half)
    angles = timesteps.astype(jnp.float32)[:, None] * freqs[None, :]
    emb = jnp.concatenate([jnp.cos(angles), jnp.sin(angles)], axis=1).astype(jnp.bfloat16)
    cond = jax.nn.silu(jnp.dot(emb, t_weight, preferred_element_type=jnp.float32)).astype(jnp.bfloat16)
    mod = jnp.dot(cond, ada_weight, preferred_element_type=jnp.float32)
    tokmod = mod[clip_tok]
    shift, scale, gate = (tokmod[:, :D], tokmod[:, D:2 * D], tokmod[:, 2 * D:])
    xf = packed.astype(jnp.float32)
    mean = lax.optimization_barrier(jnp.mean(xf, axis=1, keepdims=True))
    var = lax.optimization_barrier(jnp.mean((xf - mean) ** 2, axis=1, keepdims=True))
    h = ((xf - mean) * lax.rsqrt(var + 1e-06) * (1.0 + scale) + shift).astype(jnp.bfloat16)
    qkv = jnp.dot(h, w_qkv.reshape(D, 3 * D), preferred_element_type=jnp.float32).reshape(TOKENS, 3, D)
    q = qkv[:, 0].astype(jnp.bfloat16).reshape(TOKENS, HEADS, HEAD).transpose(1, 0, 2)
    k = qkv[:, 1].astype(jnp.bfloat16).reshape(TOKENS, HEADS, HEAD).transpose(1, 0, 2)
    v = qkv[:, 2].astype(jnp.bfloat16).reshape(TOKENS, HEADS, HEAD).transpose(1, 0, 2)
    inv = 1.0 / math.sqrt(HEAD)

    def one_head(args):
        qh, kh, vh = args
        kf = kh.astype(jnp.float32)
        vf = vh.astype(jnp.float32)

        def one_block(start):
            qb = lax.dynamic_slice_in_dim(qh, start, S_DEV, 0).astype(jnp.float32)
            cb = lax.dynamic_slice_in_dim(clip_tok, start, S_DEV, 0)
            scores = jnp.dot(qb, kf.T) * inv
            allowed = cb[:, None] == clip_tok[None, :]
            top = lax.optimization_barrier(jnp.max(jnp.where(allowed, scores, -jnp.inf), axis=1, keepdims=True))
            weights = jnp.where(allowed, jnp.exp(scores - top), 0.0)
            total = lax.optimization_barrier(jnp.sum(weights, axis=1, keepdims=True))
            rounded = weights.astype(jnp.bfloat16).astype(jnp.float32)
            return jnp.dot(rounded, vf) / total
        starts = jnp.arange(N_SEQ, dtype=jnp.int32) * S_DEV
        return lax.map(one_block, starts).reshape(TOKENS, HEAD)
    heads = lax.map(one_head, (q, k, v))
    attended = heads.transpose(1, 0, 2).reshape(TOKENS, D).astype(jnp.bfloat16)
    branch = jnp.dot(attended, w_out, preferred_element_type=jnp.float32)
    gated = gate * branch
    return (gated.astype(jnp.bfloat16), (xf + gated).astype(jnp.bfloat16))
```

```python
import functools
import math

import jax
import jax.numpy as jnp
from jax import lax
from jax.experimental import pallas as pl
from jax.experimental.pallas import tpu as pltpu
from jax.sharding import PartitionSpec as P

HEAD = 128
TILE = 256
KEYS = 512


def clip_ids(clip_blocks, positions, blk):
    ends = jnp.cumsum(clip_blocks)
    block = positions // blk
    return jnp.sum((block[:, None] >= ends[None, :]).astype(jnp.int32), axis=1)


def local(x_enc, clip_blocks, timesteps, plan_block, plan_slot, t_weight, ada_weight, w_qkv, w_out):
    nseq = lax.axis_size("seq")
    nmp = lax.axis_size("mp")
    rows, width = x_enc.shape
    blk = rows // nseq
    outgoing = x_enc.reshape(nseq, blk, width)[plan_block[0]]
    incoming = lax.all_to_all(outgoing, "seq", split_axis=0, concat_axis=0, tiled=True)
    packed = jnp.zeros_like(incoming).at[plan_slot[0]].set(incoming).reshape(rows, width)
    first_row = lax.axis_index("seq") * rows
    query_clip = clip_ids(clip_blocks, first_row + jnp.arange(rows, dtype=jnp.int32), blk)
    half = t_weight.shape[0] // 2
    freqs = jnp.exp(-math.log(10000.0) * jnp.arange(half, dtype=jnp.float32) / half)
    angles = timesteps.astype(jnp.float32)[:, None] * freqs[None, :]
    emb = jnp.concatenate([jnp.cos(angles), jnp.sin(angles)], axis=1).astype(jnp.bfloat16)
    cond = jax.nn.silu(jnp.dot(emb, t_weight, preferred_element_type=jnp.float32)).astype(
        jnp.bfloat16
    )
    ada_rows = ada_weight.shape[0]
    cond_part = lax.dynamic_slice_in_dim(
        cond, lax.axis_index(("seq", "mp")) * ada_rows, ada_rows, 1
    )
    mod = lax.psum(
        jnp.dot(cond_part, ada_weight, preferred_element_type=jnp.float32), ("seq", "mp")
    )
    clips = mod.shape[0]
    onehot = (query_clip[:, None] == jnp.arange(clips, dtype=jnp.int32)[None, :]).astype(
        jnp.float32
    )
    tokmod = jnp.dot(onehot, mod, precision=lax.Precision.HIGHEST)
    shift, scale, gate = (tokmod[:, :width], tokmod[:, width : 2 * width], tokmod[:, 2 * width :])
    xf = packed.astype(jnp.float32)
    mean = jnp.mean(xf, axis=1, keepdims=True)
    var = jnp.mean((xf - mean) ** 2, axis=1, keepdims=True)
    h = ((xf - mean) * lax.rsqrt(var + 1e-06) * (1.0 + scale) + shift).astype(jnp.bfloat16)
    cols = w_qkv.shape[2]
    qkv = jnp.dot(h, w_qkv.reshape(width, 3 * cols), preferred_element_type=jnp.float32).reshape(
        rows, 3, cols
    )
    query = qkv[:, 0].astype(jnp.bfloat16)
    keys = qkv[:, 1].astype(jnp.bfloat16)
    values = qkv[:, 2].astype(jnp.bfloat16)
    heads = cols // HEAD
    query_heads = query.reshape(rows, heads, HEAD)
    inv = 1.0 / math.sqrt(HEAD)

    def attend(carry, key_block, value_block, key_clip):
        top, total, accum = carry
        scores = (
            jnp.einsum("qhd,khd->hqk", query_heads, key_block, preferred_element_type=jnp.float32)
            * inv
        )
        allowed = (query_clip[:, None] == key_clip[None, :])[None]
        block_top = jnp.max(jnp.where(allowed, scores, -1e30), axis=2)
        new_top = jnp.maximum(top, block_top)
        weights = jnp.where(allowed, jnp.exp(scores - new_top[:, :, None]), 0.0)
        factor = jnp.exp(top - new_top)
        new_total = total * factor + jnp.sum(weights, axis=2)
        new_accum = accum * factor[:, :, None] + jnp.einsum(
            "hqk,khd->hqd",
            weights.astype(jnp.bfloat16),
            value_block,
            preferred_element_type=jnp.float32,
        )
        return (new_top, new_total, new_accum)

    init = (
        jnp.full((heads, rows), -1e30, jnp.float32),
        jnp.zeros((heads, rows), jnp.float32),
        jnp.zeros((heads, rows, HEAD), jnp.float32),
    )
    all_keys, all_values = (
        lax.all_gather(keys, "seq", axis=0, tiled=True),
        lax.all_gather(values, "seq", axis=0, tiled=True),
    )
    carry = init
    count = all_keys.shape[0] // rows
    key_stack = all_keys.reshape(count, rows, heads, HEAD)
    value_stack = all_values.reshape(count, rows, heads, HEAD)
    starts = jnp.arange(count, dtype=jnp.int32) * rows

    def step(state, item):
        key_block, value_block, block_start = item
        key_clip = clip_ids(clip_blocks, block_start + jnp.arange(rows, dtype=jnp.int32), blk)
        state = attend(state, key_block, value_block, key_clip)
        return (state, None)

    carry, _ = lax.scan(step, carry, (key_stack, value_stack, starts))
    top, total, accum = carry
    attended = (
        (accum / total[:, :, None]).transpose(1, 0, 2).reshape(rows, cols).astype(jnp.bfloat16)
    )
    share = rows // nmp
    branch = lax.psum_scatter(
        jnp.dot(attended, w_out, preferred_element_type=jnp.float32).astype(jnp.bfloat16),
        "mp",
        scatter_dimension=0,
        tiled=True,
    ).astype(jnp.float32)
    own = lax.axis_index("mp") * share
    gate_rows = lax.dynamic_slice_in_dim(gate, own, share, 0)
    x_rows = lax.dynamic_slice_in_dim(xf, own, share, 0)
    gated = gate_rows * branch
    return (gated.astype(jnp.bfloat16), (x_rows + gated).astype(jnp.bfloat16))


def project_kernel(info, p0, p1, p2, p3, mod_ref, w_ref, kv_ref, q_ref, h_ref, hq_ref, *, blk, kv_steps):
    width = h_ref.shape[1]
    part = p0.shape[0]
    group = 16
    blocks = h_ref.shape[0] // blk
    step = pl.program_id(0)

    @pl.when(step == 0)
    def _():
        for which, piece in enumerate((p0, p1, p2, p3)):
            base = info[blocks + 2 + which]

            def rows(i, _, piece=piece, base=base):
                clip = info[base * (part // blk) + i // (blk // group)]
                at = pl.multiple_of(i * group, group)
                x = piece[pl.ds(at, group), :].astype(jnp.float32)
                mean = jnp.mean(x, axis=1, keepdims=True)
                x = x - mean
                var = jnp.mean(x * x, axis=1, keepdims=True)
                shift = mod_ref[pl.ds(clip, 1), 0:width]
                scale = mod_ref[pl.ds(clip, 1), width : 2 * width]
                h = x * lax.rsqrt(var + 1e-06) * (1.0 + scale) + shift
                to = pl.multiple_of(base * part + i * group, group)
                h_ref[pl.ds(to, group), :] = h.astype(jnp.bfloat16)
                return 0

            lax.fori_loop(0, part // group, rows, 0)
        for k in range(2):
            at = pl.multiple_of(info[blocks + k] * blk, blk)
            hq_ref[pl.ds(k * blk, blk), :] = h_ref[pl.ds(at, blk), :]

    @pl.when(step < kv_steps)
    def _():
        kv_ref[...] = jnp.dot(
            h_ref[...], w_ref[0], preferred_element_type=jnp.float32
        ).astype(jnp.bfloat16)

    @pl.when(step >= kv_steps)
    def _():
        q_ref[...] = jnp.dot(
            hq_ref[...], w_ref[0], preferred_element_type=jnp.float32
        ).astype(jnp.bfloat16)


def project(info, pieces, at, mod, w3, blk):
    part, width = 128, pieces[0].shape[1]
    cols = w3.shape[2]
    per = cols // TILE
    kv_steps = 2 * per
    rows = 4 * part

    def w_map(j, info):
        return (lax.rem(lax.div(j, per) + 1, 3), 0, lax.rem(j, per))

    def piece_map(which):
        return lambda j, info: (info[at + which], 0)

    return pl.pallas_call(
        functools.partial(project_kernel, blk=blk, kv_steps=kv_steps),
        grid_spec=pltpu.PrefetchScalarGridSpec(
            num_scalar_prefetch=1,
            grid=(kv_steps + per,),
            in_specs=[pl.BlockSpec((part, width), piece_map(i)) for i in range(4)]
            + [
                pl.BlockSpec(mod.shape, lambda j, info: (0, 0)),
                pl.BlockSpec((1, width, TILE), w_map),
            ],
            out_specs=[
                pl.BlockSpec((rows, TILE), lambda j, info: (0, jnp.minimum(j, kv_steps - 1))),
                pl.BlockSpec((2 * blk, TILE), lambda j, info: (0, jnp.maximum(j - kv_steps, 0))),
            ],
            scratch_shapes=[
                pltpu.VMEM((rows, width), jnp.bfloat16),
                pltpu.VMEM((2 * blk, width), jnp.bfloat16),
            ],
        ),
        out_shape=(
            jax.ShapeDtypeStruct((rows, 2 * cols), jnp.bfloat16),
            jax.ShapeDtypeStruct((2 * blk, cols), jnp.bfloat16),
        ),
        name="project",
    )(info, *pieces, mod, w3)


def attend_kernel(info, *refs, blk, sources, first):
    q_in, k_in, v_in = refs[:sources], refs[sources : 2 * sources], refs[2 * sources : 3 * sources]
    o_ref, qs, ks, vs = refs[3 * sources :]
    per = k_in[0].shape[0] // blk
    keys = ks.shape[0]
    part = o_ref.shape[0]
    mine = part // blk
    start = info[first]
    for i in range(sources):
        slot = info[sources * per + i]
        qs[pl.ds(pl.multiple_of(slot * blk, blk), blk), :] = q_in[i][...]
        for b in range(per):
            to = pl.multiple_of(info[i * per + b] * blk, blk)
            ks[pl.ds(to, blk), :] = k_in[i][b * blk : (b + 1) * blk, :]
            vs[pl.ds(to, blk), :] = v_in[i][b * blk : (b + 1) * blk, :]
    ranges = sources * per + sources
    query = qs[pl.ds(pl.multiple_of(start * blk, blk), part), :]
    row = lax.broadcasted_iota(jnp.int32, (part, 1), 0)
    low = jnp.zeros((part, 1), jnp.int32)
    high = jnp.zeros((part, 1), jnp.int32)
    for j in range(mine):
        here = (row >= j * blk) & (row < (j + 1) * blk)
        low = jnp.where(here, info[ranges + start + j], low)
        high = jnp.where(here, info[ranges + sources + start + j], high)
    begin = info[ranges + start]
    end = info[ranges + sources + start + mine - 1]
    inv = 1.0 / math.sqrt(HEAD)

    def body(t, carry):
        top, total, accum = carry
        want = begin + t * KEYS
        base = pl.multiple_of(jnp.minimum(want, keys - KEYS), blk)
        key = ks[pl.ds(base, KEYS), :]
        value = vs[pl.ds(base, KEYS), :]
        scores = lax.dot_general(
            query, key, (((1,), (1,)), ((), ())), preferred_element_type=jnp.float32
        )
        at = base + lax.broadcasted_iota(jnp.int32, (1, KEYS), 1)
        allowed = (at >= jnp.maximum(low, want)) & (at < high)
        scores = jnp.where(allowed, scores, -1e30)
        new_top = jnp.maximum(top, jnp.max(scores, axis=1, keepdims=True))
        weights = jnp.exp((scores - new_top) * inv)
        factor = jnp.exp((top - new_top) * inv)
        total = total * factor + jnp.sum(weights, axis=1, keepdims=True)
        accum = accum * factor + jnp.dot(
            weights.astype(jnp.bfloat16), value, preferred_element_type=jnp.float32
        )
        return new_top, total, accum

    carry = (
        jnp.full((part, 1), -1e30, jnp.float32),
        jnp.zeros((part, 1), jnp.float32),
        jnp.zeros((part, HEAD), jnp.float32),
    )
    _, total, accum = lax.fori_loop(0, lax.div(end - begin + KEYS - 1, KEYS), body, carry)
    o_ref[...] = (accum / total).astype(jnp.bfloat16)


def attend(info, first, queries, kvs, part, blk):
    sources = len(kvs)
    rows, cols = kvs[0].shape[0], kvs[0].shape[1] // 2
    heads = cols // HEAD
    keys = sources * rows
    q_spec = pl.BlockSpec((blk, HEAD), lambda h, info: (0, h))
    k_spec = pl.BlockSpec((rows, HEAD), lambda h, info: (0, h))
    v_spec = pl.BlockSpec((rows, HEAD), lambda h, info: (0, heads + h))
    return pl.pallas_call(
        functools.partial(attend_kernel, blk=blk, sources=sources, first=first),
        grid_spec=pltpu.PrefetchScalarGridSpec(
            num_scalar_prefetch=1,
            grid=(heads,),
            in_specs=[q_spec] * sources + [k_spec] * sources + [v_spec] * sources,
            out_specs=pl.BlockSpec((part, HEAD), lambda h, info: (0, h)),
            scratch_shapes=[
                pltpu.VMEM((sources * blk, HEAD), jnp.bfloat16),
                pltpu.VMEM((keys, HEAD), jnp.bfloat16),
                pltpu.VMEM((keys, HEAD), jnp.bfloat16),
            ],
        ),
        out_shape=jax.ShapeDtypeStruct((part, cols), jnp.bfloat16),
        name="attend",
    )(info, *queries, *kvs, *kvs)


def modulation(timesteps, t_weight, ada_weight, plan_block, plan_slot, nseq, nmp):
    devices = nseq * nmp
    half = t_weight.shape[0] // 2
    freqs = jnp.exp(-math.log(10000.0) * jnp.arange(half, dtype=jnp.float32) / half)
    angles = timesteps.astype(jnp.float32)[:, None] * freqs[None, :]
    emb = jnp.concatenate([jnp.cos(angles), jnp.sin(angles)], axis=1).astype(jnp.bfloat16)
    cond = jax.nn.silu(jnp.dot(emb, t_weight, preferred_element_type=jnp.float32)).astype(
        jnp.bfloat16
    )
    ada_rows = ada_weight.shape[0]
    cond_part = lax.dynamic_slice_in_dim(
        cond, lax.axis_index(("seq", "mp")) * ada_rows, ada_rows, 1
    )
    part = jnp.dot(cond_part, ada_weight, preferred_element_type=jnp.float32)
    clips, total = part.shape
    own = total // devices
    part = part.reshape(clips, devices, own).transpose(1, 0, 2)
    part = lax.all_to_all(part, ("seq", "mp"), split_axis=0, concat_axis=0, tiled=True)
    summed = jnp.sum(part, axis=0)
    plans = jnp.concatenate([plan_block, plan_slot], axis=0).astype(jnp.float32)
    plans = jnp.pad(plans, ((0, clips - 2), (0, 0)))
    own_all = jnp.concatenate([summed, plans], axis=1)
    shared = lax.all_to_all(
        jnp.broadcast_to(own_all[None], (devices,) + own_all.shape),
        ("seq", "mp"),
        split_axis=0,
        concat_axis=0,
        tiled=True,
    )
    mod = shared[:, :, :own].transpose(1, 0, 2).reshape(clips, total)
    plans = shared.reshape(nseq, nmp, clips, -1)[:, 0, :2, own:].astype(jnp.int32)
    return mod, plans[:, 0], plans[:, 1]


def line(x_enc, clip_blocks, timesteps, plan_block, plan_slot, t_weight, ada_weight, w_qkv, w_out):
    nseq, nmp = lax.axis_size("seq"), lax.axis_size("mp")
    rows, width = x_enc.shape
    blk = rows // nseq
    layers, part = nseq // 2, 128
    half = rows // nmp
    subs = half // part
    seq, mp = lax.axis_index("seq"), lax.axis_index("mp")
    layer, core = seq // 2, seq % 2
    middle = (layer == 1) | (layer == 2)

    def hop(x, pairs):
        return lax.ppermute(
            x, "seq", [(2 * a + c, 2 * b + c) for a, b in pairs for c in range(2)]
        )

    def across(x):
        return lax.ppermute(x, "mp", [(0, 1), (1, 0)])

    def beside(x):
        return lax.ppermute(x, "seq", [(i, i ^ 1) for i in range(nseq)])

    near = ((0, 1), (1, 0), (2, 3), (3, 2))
    inner = ((1, 2), (2, 1))
    outer = ((1, 0), (2, 3))
    own = [lax.dynamic_slice_in_dim(x_enc, mp * half + part * i, part, 0) for i in range(subs)]
    first = [hop(x, near) for x in own]
    across_mid = [hop(x, inner) for x in own]
    first_far = [across(x) for x in first]
    second = [jnp.where(middle, a, hop(a, outer)) for a in across_mid]
    second_far = [across(x) for x in second]
    onward = [hop(x, inner) for x in first]
    third = [jnp.where(middle, a, hop(a, outer)) for a in onward]
    third_far = [across(x) for x in third]

    mod, blocks_of, slots_of = modulation(
        timesteps, t_weight, ada_weight, plan_block, plan_slot, nseq, nmp
    )
    ends = jnp.cumsum(clip_blocks)
    begins = ends - clip_blocks
    total_blocks = nseq * nseq
    order = jnp.arange(total_blocks, dtype=jnp.int32)
    clip_of = jnp.sum((order[:, None] >= ends[None, :]).astype(jnp.int32), axis=1)
    dest = jnp.arange(nseq, dtype=jnp.int32)
    place = (dest[:, None] * nseq + slots_of).T
    is_block = blocks_of[:, :, None] == dest[None, None, :]
    where_to = jnp.sum(jnp.where(is_block, place[:, :, None], 0), axis=1)
    clip_at = jnp.sum(
        jnp.where(where_to[:, :, None] == order[None, None, :], clip_of[None, None, :], 0), axis=2
    )
    low_side = layer < 2
    layer_of = [
        layer,
        layer ^ 1,
        jnp.where(low_side, 2, 1),
        jnp.where(low_side, 3, 0),
    ]
    w3 = jnp.transpose(w_qkv, (1, 0, 2))
    halves = [mp * subs + i for i in range(subs)] + [(1 - mp) * subs + i for i in range(subs)]
    kvs, far_kvs, qs, far_qs, xs, far_xs = [], [], [], [], [], []
    groups = [
        [x_enc] * 4,
        first + first_far,
        second + second_far,
        third + third_far,
    ]
    for i, pieces in enumerate(groups):
        source = 2 * layer_of[i] + core
        wanted = jnp.stack([blocks_of[source, seq], blocks_of[source, seq ^ 1]])
        info = jnp.concatenate(
            [clip_at[source], wanted, jnp.stack(halves), jnp.zeros((4,), jnp.int32)]
        ).astype(jnp.int32)
        at = nseq + 2 if i == 0 else nseq + 6
        kv, q = project(info, pieces, at, mod, w3, blk)
        kvs.append(kv)
        far_kvs.append(beside(kv))
        qs.append(q[:blk])
        far_qs.append(beside(q[blk:]))
        if i == 0:
            full = x_enc
        else:
            full = jnp.zeros_like(x_enc)
            for h, p in zip(halves, pieces):
                full = lax.dynamic_update_slice_in_dim(full, p, h * part, 0)
        xs.append(lax.dynamic_slice_in_dim(full, wanted[0] * blk, blk, 0))
        far_xs.append(beside(lax.dynamic_slice_in_dim(full, wanted[1] * blk, blk, 0)))
    origins = jnp.stack(
        [2 * a + core for a in layer_of] + [2 * a + 1 - core for a in layer_of]
    )
    my_slots = slots_of[seq][origins]
    mine = seq * nseq + dest
    my_clip = clip_of[mine]
    share = rows // nmp
    per_share = share // blk
    table = jnp.concatenate(
        [
            where_to[origins].reshape(-1),
            my_slots,
            begins[my_clip] * blk,
            ends[my_clip] * blk,
            jnp.stack([(1 - mp) * per_share, mp * per_share]),
        ]
    ).astype(jnp.int32)
    first_at = total_blocks + 3 * nseq
    away = attend(table, first_at, qs + far_qs, kvs + far_kvs, share, blk)
    sent = across(jnp.dot(away, w_out, preferred_element_type=jnp.float32).astype(jnp.bfloat16))
    home = attend(table, first_at + 1, qs + far_qs, kvs + far_kvs, share, blk)
    branch = jnp.dot(home, w_out, preferred_element_type=jnp.float32)
    branch = branch + sent.astype(jnp.float32)
    gate = mod[:, 2 * width :]
    slot = mp * per_share + jnp.arange(per_share, dtype=jnp.int32)
    onehot = (my_slots[None, :] == slot[:, None]).astype(jnp.int32)
    pick = jnp.sum(onehot * dest[None, :], axis=1)
    x_rows = jnp.stack(xs + far_xs)[pick].reshape(share, width).astype(jnp.float32)
    row_gate = gate[my_clip[slot]]
    gated = (row_gate[:, None, :] * branch.reshape(per_share, blk, width)).reshape(share, width)
    return (gated.astype(jnp.bfloat16), (x_rows + gated).astype(jnp.bfloat16))


def solution(mesh):
    body = line if (mesh.shape["seq"], mesh.shape["mp"]) == (8, 2) else local
    return jax.shard_map(
        body,
        mesh=mesh,
        in_specs=(
            P(("dp", "seq"), None),
            P("dp"),
            P("dp"),
            P(("dp", "seq"), None),
            P(("dp", "seq"), None),
            P(),
            P(("seq", "mp"), None),
            P(None, None, "mp"),
            P("mp", None),
        ),
        out_specs=(P(("dp", "seq", "mp"), None), P(("dp", "seq", "mp"), None)),
        check_vma=False,
    )
```
